1024 devices in a mesh: row: 32 (over z), col: 32 (over y, x, core).
Axes of the slice: x: 4, y: 4, z: 32, core: 2. Of those that a mesh axis runs over, the one named last changes fastest.
Arguments:
- momentum: float32 [8192, 28672], P('row', 'col'), may hold values from -400 to 400, as said below
- gradient: bfloat16 [8192, 28672], P('row', 'col'), may hold values from -3 to 3
- right_prev: float32 [28672, 256], P('col'), may hold values from -5 to 5
Outputs:
- new_momentum: float32 [8192, 28672], P('row', 'col')
- right_next: float32 [28672, 256], P('col')
- update: bfloat16 [8192, 28672], P('row', 'col')
The draws below stay inside these ranges and needn't reach their ends.
Inputs may be any that keep to these rules, and one draw needn't show every extreme that they name: momentum entries are finite reals.
All inputs are finite; a program needn't handle non-finite values.
Results may differ from the reference program's by a relative error of at most 0.001.
Values sent between devices are 32-bit elements; how exact they have to be, the bound alone decides.
No kernel may reach another device: no remote copies, remote signals or barrier semaphores. Data moves between devices by JAX's collectives and lax.ppermute only.
A program may use at most 32 MiB of HBM per device.

```python
import math
import jax
import jax.numpy as jnp
from jax import lax

D = 8192
FF = 28672
RANK = 256


def draw_momentum(key, part):
    keys = jax.random.split(key, 3)
    rowpos = jnp.arange(D, dtype=jnp.float32)[:, None] / D
    colpos = jnp.arange(FF, dtype=jnp.float32)[None, :] / FF
    rise = 3.0
    values = jnp.clip(jax.random.normal(keys[0], (D, FF), jnp.float32), -5.0, 5.0)
    row_scale = jnp.exp(rowpos * math.log(rise) + jax.random.uniform(keys[1], (D, 1), jnp.float32, 0.0, math.log(3.2)))
    col_scale = jnp.exp(colpos * math.log(rise) + jax.random.uniform(keys[2], (1, FF), jnp.float32, 0.0, math.log(3.2)))
    return 0.3 * values * row_scale * col_scale


def level_of(stream_key, shape, cuts, least, largest):
    factor_of, own = 1.0, jax.random.fold_in(stream_key, 6)
    for axis_at, blocks in cuts:
        steps = jnp.exp(jax.random.uniform(jax.random.fold_in(own, axis_at), (blocks,), jnp.float32, least / len(cuts), largest / len(cuts)))
        factor_of = factor_of * jnp.repeat(steps, shape[axis_at] // blocks).reshape([-1 if axis == axis_at else 1 for axis in range(len(shape))])
    return factor_of


def bell_draw(rng, shape, width, limit, cuts=(), held_as=jnp.bfloat16):
    entries = width * jax.random.normal(rng, shape, jnp.float32)
    if cuts:
        entries = entries * level_of(rng, shape, cuts, -0.22, 0.18)
    return jnp.clip(entries, -limit, limit).astype(held_as)


def setup_inputs(seed: int = 0) -> dict:
    splits = jax.random.split(jax.random.key(seed), 4)
    return {
        "momentum": draw_momentum(jax.random.fold_in(splits[3], 71), 0),
        "gradient": bell_draw(splits[1], (D, FF), 0.5, 3.0, ((0, 32), (1, 32))),
        "right_prev": bell_draw(splits[2], (FF, RANK), 1.0, 5.0, ((0, 32),), jnp.float32),
    }


HI = lax.Precision.HIGHEST

def reference(momentum, gradient, right_prev):
    merged = momentum + gradient.astype(jnp.float32)
    left = jnp.dot(merged.astype(jnp.float32), right_prev.astype(jnp.float32), precision=HI, preferred_element_type=jnp.float32)
    gram = jnp.dot(left.T.astype(jnp.float32), left.astype(jnp.float32), precision=HI, preferred_element_type=jnp.float32)
    chol = jnp.linalg.cholesky(gram)
    ortho = jax.scipy.linalg.solve_triangular(chol, left.T, lower=True).T
    right = jnp.dot(merged.T.astype(jnp.float32), ortho.astype(jnp.float32), precision=HI, preferred_element_type=jnp.float32)
    colsq = lax.optimization_barrier(jnp.sum(right * right, axis=0))
    right_next = right * lax.rsqrt(colsq / FF + 1e-06)
    new_momentum = merged - 0.05 * jnp.dot(ortho.astype(jnp.float32), right.T.astype(jnp.float32), precision=HI, preferred_element_type=jnp.float32)
    factor = jnp.sqrt(jnp.float32(D) / jnp.float32(RANK))
    update = (factor * jnp.dot(ortho.astype(jnp.float32), right_next.T.astype(jnp.float32), precision=HI, preferred_element_type=jnp.float32)).astype(jnp.bfloat16)
    return (new_momentum, right_next, update)
```

```python
import jax
import jax.numpy as jnp
from jax import lax
from jax.sharding import Mesh, PartitionSpec as P

HI = lax.Precision.HIGHEST
NEAR = 4
FAR_AXIS, NEAR_AXIS, COL = "far", "near", "col"


def dot(a, b, contract):
    return lax.dot_general(
        a, b, ((contract[:1], contract[1:]), ((), ())), precision=HI, preferred_element_type=jnp.float32
    )


def exchange(blocks, axis):
    return lax.all_to_all(blocks, axis, 0, 0)


def on_device(far, cols, momentum, gradient, right_prev):
    near = NEAR
    rows, width = momentum.shape
    rank = right_prev.shape[1]
    depth, full_width = far * near * rows, cols * width
    step, part = rank // (far * near), rank // cols
    merged = momentum + gradient.astype(jnp.float32)

    local = dot(right_prev, merged, (0, 1))
    block = exchange(local.reshape(cols, part, rows), COL).sum(0)
    left = lax.all_gather(block, COL, axis=0, tiled=True)

    gram_block = dot(block, left, (1, 1))
    shuffled = left.reshape(far, near, step, rows).transpose(1, 0, 2, 3).reshape(rank, rows)
    raw = dot(shuffled, merged, (1, 0)).reshape(near, far * step, width)
    extra = jnp.pad(gram_block, ((0, 0), (0, width - rank)))
    sent = jnp.concatenate([raw, jnp.broadcast_to(extra[None], (near, part, width))], axis=1)
    got = exchange(sent, NEAR_AXIS).sum(0)
    raw = got[: far * step].reshape(far, step, width)
    gram_block = got[far * step :, :rank]
    sent = jnp.concatenate([raw, jnp.broadcast_to(gram_block[None], (far, part, rank))], axis=2)
    got = exchange(sent, FAR_AXIS).sum(0)
    raw_block, gram_block = got[:, :width], got[:, width:]
    gram = exchange(jnp.broadcast_to(gram_block[None], (cols, part, rank)), COL).reshape(rank, rank)
    raw = lax.all_gather(raw_block, (FAR_AXIS, NEAR_AXIS), axis=0, tiled=True)

    chol = jnp.linalg.cholesky(gram)
    inverse = jax.scipy.linalg.solve_triangular(chol, jnp.eye(rank, dtype=jnp.float32), lower=True)
    ortho = dot(inverse, left, (1, 0))
    right = dot(raw, inverse, (0, 1))
    colsq = lax.all_gather(jnp.sum(right * right, axis=0), COL, axis=0).sum(0)
    right_next = right * lax.rsqrt(colsq / full_width + 1e-06)
    new_momentum = merged - 0.05 * dot(ortho, right, (0, 1))
    factor = jnp.sqrt(jnp.float32(depth) / jnp.float32(rank))
    update = (factor * dot(ortho, right_next, (0, 1))).astype(jnp.bfloat16)
    return (new_momentum, right_next, update)


def solution(mesh):
    row, cols = mesh.devices.shape
    far = row // NEAR
    split = Mesh(mesh.devices.reshape(far, NEAR, cols), (FAR_AXIS, NEAR_AXIS, COL))
    both = P((FAR_AXIS, NEAR_AXIS), COL)
    side = P(COL, None)

    def step(momentum, gradient, right_prev):
        return on_device(far, cols, momentum, gradient, right_prev)

    return jax.shard_map(
        step, mesh=split, in_specs=(both, both, side), out_specs=(both, side, both), check_vma=False
    )
```

```python
import jax
import jax.numpy as jnp
from jax import lax
from jax.experimental import pallas as pl
from jax.experimental.pallas import tpu as pltpu
from jax.sharding import Mesh, PartitionSpec as P

HI = lax.Precision.HIGHEST
NEAR = 4
FAR_AXIS, NEAR_AXIS, COL = "far", "near", "col"


def dot(a, b, contract):
    return lax.dot_general(
        a, b, ((contract[:1], contract[1:]), ((), ())), precision=HI, preferred_element_type=jnp.float32
    )


def invert64(block):
    row = lax.broadcasted_iota(jnp.int32, (64, 128), 0)
    lane = lax.broadcasted_iota(jnp.int32, (64, 128), 1)
    sub8 = lax.broadcasted_iota(jnp.int32, (8, 128), 0)
    lane8 = lax.broadcasted_iota(jnp.int32, (8, 128), 1)
    state = jnp.where(lane < 64, block, jnp.where(lane - 64 == row, 1.0, 0.0))

    def eight(k, state):
        tile = state[:8]
        columns = [jnp.broadcast_to(tile[:, i : i + 1], (8, 128)) for i in range(8)]
        scale = jnp.zeros((8, 128), jnp.float32)
        for i in range(8):
            inverse = 1.0 / jnp.broadcast_to(columns[i][i : i + 1], (8, 128))
            scale = jnp.where(sub8 == i, inverse, scale)
            factor = jnp.where(sub8 > i, columns[i] * inverse, 0.0)
            for j in range(i + 1, 8):
                columns[j] = columns[j] - factor * jnp.broadcast_to(columns[j][i : i + 1], (8, 128))
            tile = tile - factor * jnp.broadcast_to(tile[i : i + 1], (8, 128))
        open_lanes = (lane8 >= 8) & (lane8 < 64 - 8 * k)
        factor = jnp.where(open_lanes, tile * scale, 0.0)[:, :64]
        rest = state[8:] - dot(factor, tile, (0, 0))[8:]
        done = tile * jnp.sqrt(scale)
        return pltpu.roll(jnp.concatenate([rest, done], axis=0), 120, 1)

    state = lax.fori_loop(0, 8, eight, state)
    return jnp.where(lane < 64, state, 0.0)


def tall(x):
    return jnp.concatenate([x, jnp.zeros_like(x)], axis=0)


def invert128(block):
    first = invert64(block[:64])
    first_tall = tall(first)
    below = dot(block[64:], first_tall, (1, 1))
    rest = pltpu.roll(block[64:], 64, 1) - dot(below, tall(below), (1, 1))
    second = invert64(rest)
    corner = dot(second, tall(dot(below, first_tall, (1, 0))), (1, 0))
    return jnp.concatenate([first, pltpu.roll(second, 64, 1) - corner], axis=0)


def invert_kernel(gram_ref, out_ref):
    first = invert128(gram_ref[:128, :128])
    below = dot(gram_ref[128:, :128], first, (1, 1))
    second = invert128(gram_ref[128:, 128:] - dot(below, below, (1, 1)))
    out_ref[:128, :128] = first
    out_ref[:128, 128:] = jnp.zeros((128, 128), jnp.float32)
    out_ref[128:, :128] = -dot(second, dot(below, first, (1, 0)), (1, 0))
    out_ref[128:, 128:] = second


def inverse_factor(gram):
    return pl.pallas_call(
        invert_kernel,
        out_shape=jax.ShapeDtypeStruct((256, 256), jnp.float32),
        in_specs=[pl.BlockSpec(memory_space=pltpu.VMEM)],
        out_specs=pl.BlockSpec(memory_space=pltpu.VMEM),
        cost_estimate=pl.CostEstimate(flops=10_000_000_000, bytes_accessed=50_000_000, transcendentals=0),
    )(gram)


def exchange(blocks, axis):
    return lax.all_to_all(blocks, axis, 0, 0)


def collect(block, count, axis):
    return exchange(jnp.broadcast_to(block[None], (count, *block.shape)), axis)


def on_device(far, cols, momentum, gradient, right_prev):
    near = NEAR
    rows, width = momentum.shape
    rank = right_prev.shape[1]
    depth, full_width = far * near * rows, cols * width
    step, part = rank // (far * near), rank // cols
    merged = momentum + gradient.astype(jnp.float32)

    local = dot(right_prev, merged, (0, 1))
    block = exchange(local.reshape(cols, part, rows), COL).sum(0)
    left = collect(block, cols, COL).reshape(rank, rows)

    gram_block = dot(block, left, (1, 1))
    raw = dot(left, merged, (1, 0)).reshape(near, far * step, width)
    extra = jnp.pad(gram_block, ((0, 0), (0, width - rank)))
    sent = jnp.concatenate([raw, jnp.broadcast_to(extra[None], (near, part, width))], axis=1)
    got = exchange(sent, NEAR_AXIS).sum(0)
    raw = got[: far * step].reshape(far, step, width)
    gram_block = got[far * step :, :rank]
    sent = jnp.concatenate([raw, jnp.broadcast_to(gram_block[None], (far, part, rank))], axis=2)
    got = exchange(sent, FAR_AXIS).sum(0)
    raw_block, gram_block = got[:, :width], got[:, width:]
    gram = lax.all_gather(gram_block, COL, axis=0, tiled=True)
    raw = collect(raw_block, far, FAR_AXIS).reshape(far * step, width)
    inverse = inverse_factor(gram)
    raw = lax.all_gather(raw, NEAR_AXIS, axis=0, tiled=True)

    ortho = dot(inverse, left, (1, 0))
    right = dot(raw, inverse, (0, 1))
    colsq = collect(jnp.sum(right * right, axis=0, keepdims=True), cols, COL).sum(0)
    right_next = right * lax.rsqrt(colsq / full_width + 1e-06)
    new_momentum = merged - 0.05 * dot(ortho, right, (0, 1))
    factor = jnp.sqrt(jnp.float32(depth) / jnp.float32(rank))
    update = (factor * dot(ortho, right_next, (0, 1))).astype(jnp.bfloat16)
    return (new_momentum, right_next, update)


def solution(mesh):
    row, cols = mesh.devices.shape
    far = row // NEAR
    split = Mesh(mesh.devices.reshape(far, NEAR, cols), (FAR_AXIS, NEAR_AXIS, COL))
    both = P((FAR_AXIS, NEAR_AXIS), COL)
    side = P(COL, None)

    def step(momentum, gradient, right_prev):
        return on_device(far, cols, momentum, gradient, right_prev)

    return jax.shard_map(
        step, mesh=split, in_specs=(both, both, side), out_specs=(both, side, both), check_vma=False
    )
```

```python
import jax
import jax.numpy as jnp
from jax import lax
from jax.experimental import pallas as pl
from jax.experimental.pallas import tpu as pltpu
from jax.sharding import Mesh, PartitionSpec as P

HI = lax.Precision.HIGHEST
NEAR = 4
FAR_AXIS, NEAR_AXIS, COL = AXES = "far", "near", "col"


def dot(a, b, contract, precision=HI):
    return lax.dot_general(
        a, b, ((contract[:1], contract[1:]), ((), ())), precision=precision, preferred_element_type=jnp.float32
    )


def invert64(block):
    row = lax.broadcasted_iota(jnp.int32, (64, 128), 0)
    lane = lax.broadcasted_iota(jnp.int32, (64, 128), 1)
    sub8 = lax.broadcasted_iota(jnp.int32, (8, 128), 0)
    lane8 = lax.broadcasted_iota(jnp.int32, (8, 128), 1)
    state = jnp.where(lane < 64, block, jnp.where(lane - 64 == row, 1.0, 0.0))

    def eight(k, state):
        tile = state[:8]
        columns = [jnp.broadcast_to(tile[:, i : i + 1], (8, 128)) for i in range(8)]
        scale = jnp.zeros((8, 128), jnp.float32)
        for i in range(8):
            inverse = 1.0 / jnp.broadcast_to(columns[i][i : i + 1], (8, 128))
            scale = jnp.where(sub8 == i, inverse, scale)
            factor = jnp.where(sub8 > i, columns[i] * inverse, 0.0)
            for j in range(i + 1, 8):
                columns[j] = columns[j] - factor * jnp.broadcast_to(columns[j][i : i + 1], (8, 128))
            tile = tile - factor * jnp.broadcast_to(tile[i : i + 1], (8, 128))
        open_lanes = (lane8 >= 8) & (lane8 < 64 - 8 * k)
        factor = jnp.where(open_lanes, tile * scale, 0.0)[:, :64]
        rest = state[8:] - dot(factor, tile, (0, 0))[8:]
        done = tile * jnp.sqrt(scale)
        return pltpu.roll(jnp.concatenate([rest, done], axis=0), 120, 1)

    state = lax.fori_loop(0, 8, eight, state)
    return jnp.where(lane < 64, state, 0.0)


def tall(x):
    return jnp.concatenate([x, jnp.zeros_like(x)], axis=0)


def invert128(block):
    first = invert64(block[:64])
    first_tall = tall(first)
    below = dot(block[64:], first_tall, (1, 1))
    rest = pltpu.roll(block[64:], 64, 1) - dot(below, tall(below), (1, 1))
    second = invert64(rest)
    corner = dot(second, tall(dot(below, first_tall, (1, 0))), (1, 0))
    return jnp.concatenate([first, pltpu.roll(second, 64, 1) - corner], axis=0)


def invert_kernel(gram_ref, out_ref):
    first = invert128(gram_ref[:128, :128])
    below = dot(gram_ref[128:, :128], first, (1, 1))
    second = invert128(gram_ref[128:, 128:] - dot(below, below, (1, 1)))
    out_ref[:128, :128] = first
    out_ref[:128, 128:] = jnp.zeros((128, 128), jnp.float32)
    out_ref[128:, :128] = -dot(second, dot(below, first, (1, 0)), (1, 0))
    out_ref[128:, 128:] = second


def inverse_factor(gram):
    return pl.pallas_call(
        invert_kernel,
        out_shape=jax.ShapeDtypeStruct((256, 256), jnp.float32),
        in_specs=[pl.BlockSpec(memory_space=pltpu.VMEM)],
        out_specs=pl.BlockSpec(memory_space=pltpu.VMEM),
        cost_estimate=pl.CostEstimate(flops=10_000_000_000, bytes_accessed=50_000_000, transcendentals=0),
    )(gram)


def exchange(blocks, axis):
    return lax.all_to_all(blocks, axis, 0, 0)


def near_pairs(far, cols, k):
    pairs = []
    for f in range(far):
        for a in range(NEAR):
            for col in range(cols):
                b, g = a ^ k, f
                if col % 2 and (a < 2) != (b < 2):
                    g = (f + (1 if a >= 2 else -1)) % far
                pairs.append(((f * NEAR + a) * cols + col, (g * NEAR + b) * cols + col))
    return pairs


def collect(block, count, axis):
    return exchange(jnp.broadcast_to(block[None], (count, *block.shape)), axis)


def on_device(far, cols, momentum, gradient, right_prev):
    near = NEAR
    rows, width = momentum.shape
    rank = right_prev.shape[1]
    depth, full_width = far * near * rows, cols * width
    step, part = rank // (far * near), rank // cols
    merged = momentum + gradient.astype(jnp.float32)

    local = dot(right_prev, merged, (0, 1))
    block = exchange(local.reshape(cols, part, rows), COL).sum(0)
    left = collect(block, cols, COL).reshape(rank, rows)

    gram_block = dot(block, left, (1, 1))
    raw = dot(left, merged, (1, 0)).reshape(near, far * step, width)
    extra = jnp.pad(gram_block, ((0, 0), (0, width - rank)))
    mine = lax.axis_index(NEAR_AXIS)

    def block_for(k):
        chosen = lax.dynamic_index_in_dim(raw, jnp.bitwise_xor(mine, k), 0, keepdims=False)
        return jnp.concatenate([chosen, extra], axis=0)

    got = block_for(0)
    for came in [lax.ppermute(block_for(k), AXES, near_pairs(far, cols, k)) for k in (2, 3, 1)]:
        got = got + came
    raw = got[: far * step].reshape(far, step, width)
    gram_block = got[far * step :, :rank]
    sent = jnp.concatenate([raw, jnp.broadcast_to(gram_block[None], (far, part, rank))], axis=2)
    got = exchange(sent, FAR_AXIS).sum(0)
    raw_block, gram_block = got[:, :width], got[:, width:]
    gram = lax.all_gather(gram_block, COL, axis=0, tiled=True)
    raw = collect(raw_block, far, FAR_AXIS).reshape(far * step, width)
    inverse = inverse_factor(gram)
    raw = lax.all_gather(raw, NEAR_AXIS, axis=0, tiled=True)

    ortho = dot(inverse, left, (1, 0))
    right = dot(raw, inverse, (0, 1))
    colsq = collect(jnp.sum(right * right, axis=0, keepdims=True), cols, COL).sum(0)
    right_next = right * lax.rsqrt(colsq / full_width + 1e-06)
    new_momentum = merged - 0.05 * dot(ortho, right, (0, 1), lax.Precision.HIGH)
    factor = jnp.sqrt(jnp.float32(depth) / jnp.float32(rank))
    update = (factor * dot(ortho, right_next, (0, 1), lax.Precision.HIGH)).astype(jnp.bfloat16)
    return (new_momentum, right_next, update)


def solution(mesh):
    row, cols = mesh.devices.shape
    far = row // NEAR
    split = Mesh(mesh.devices.reshape(far, NEAR, cols), (FAR_AXIS, NEAR_AXIS, COL))
    both = P((FAR_AXIS, NEAR_AXIS), COL)
    side = P(COL, None)

    def step(momentum, gradient, right_prev):
        return on_device(far, cols, momentum, gradient, right_prev)

    return jax.shard_map(
        step, mesh=split, in_specs=(both, both, side), out_specs=(both, side, both), check_vma=False
    )
```

```python
import jax
import jax.numpy as jnp
from jax import lax
from jax.experimental import pallas as pl
from jax.experimental.pallas import tpu as pltpu
from jax.sharding import Mesh, PartitionSpec as P


HI = lax.Precision.HIGHEST
NEAR = 4
FAR_AXIS, NEAR_AXIS, COL = AXES = "far", "near", "col"


def dot(a, b, contract, precision=HI):
    return lax.dot_general(
        a, b, ((contract[:1], contract[1:]), ((), ())), precision=precision, preferred_element_type=jnp.float32
    )


def invert64(block):
    row = lax.broadcasted_iota(jnp.int32, (64, 128), 0)
    lane = lax.broadcasted_iota(jnp.int32, (64, 128), 1)
    sub8 = lax.broadcasted_iota(jnp.int32, (8, 128), 0)
    lane8 = lax.broadcasted_iota(jnp.int32, (8, 128), 1)
    state = jnp.where(lane < 64, block, jnp.where(lane - 64 == row, 1.0, 0.0))

    def eight(k, state):
        tile = state[:8]
        columns = [jnp.broadcast_to(tile[:, i : i + 1], (8, 128)) for i in range(8)]
        scale = jnp.zeros((8, 128), jnp.float32)
        for i in range(8):
            inverse = 1.0 / jnp.broadcast_to(columns[i][i : i + 1], (8, 128))
            scale = jnp.where(sub8 == i, inverse, scale)
            factor = jnp.where(sub8 > i, columns[i] * inverse, 0.0)
            for j in range(i + 1, 8):
                columns[j] = columns[j] - factor * jnp.broadcast_to(columns[j][i : i + 1], (8, 128))
            tile = tile - factor * jnp.broadcast_to(tile[i : i + 1], (8, 128))
        open_lanes = (lane8 >= 8) & (lane8 < 64 - 8 * k)
        factor = jnp.where(open_lanes, tile * scale, 0.0)[:, :64]
        rest = state[8:] - dot(factor, tile, (0, 0))[8:]
        done = tile * jnp.sqrt(scale)
        return pltpu.roll(jnp.concatenate([rest, done], axis=0), 120, 1)

    state = lax.fori_loop(0, 8, eight, state)
    return jnp.where(lane < 64, state, 0.0)


def tall(x):
    return jnp.concatenate([x, jnp.zeros_like(x)], axis=0)


def invert128(block):
    first = invert64(block[:64])
    first_tall = tall(first)
    below = dot(block[64:], first_tall, (1, 1))
    rest = pltpu.roll(block[64:], 64, 1) - dot(below, tall(below), (1, 1))
    second = invert64(rest)
    corner = dot(second, tall(dot(below, first_tall, (1, 0))), (1, 0))
    return jnp.concatenate([first, pltpu.roll(second, 64, 1) - corner], axis=0)


def first_kernel(gram_ref, first_ref, carry_ref, rest_ref):
    first = invert128(gram_ref[:128, :128])
    below = dot(gram_ref[128:, :128], first, (1, 1))
    first_ref[...] = first
    carry_ref[...] = dot(below, first, (1, 0))
    rest_ref[...] = gram_ref[128:, 128:] - dot(below, below, (1, 1))


def second_kernel(first_ref, carry_ref, rest_ref, out_ref):
    second = invert128(rest_ref[...])
    out_ref[:128, :128] = first_ref[...].T
    out_ref[:128, 128:] = -dot(second, carry_ref[...], (1, 0)).T
    out_ref[128:, :128] = jnp.zeros((128, 128), jnp.float32)
    out_ref[128:, 128:] = second.T


def in_vmem(kernel, shapes, *arrays):
    return pl.pallas_call(
        kernel,
        out_shape=[jax.ShapeDtypeStruct(shape, jnp.float32) for shape in shapes],
        in_specs=[pl.BlockSpec(memory_space=pltpu.VMEM)] * len(arrays),
        out_specs=[pl.BlockSpec(memory_space=pltpu.VMEM)] * len(shapes),
        cost_estimate=pl.CostEstimate(flops=5_000_000_000, bytes_accessed=30_000_000, transcendentals=0),
    )(*arrays)


def exchange(blocks, axis):
    return lax.all_to_all(blocks, axis, 0, 0)


def near_pairs(far, cols, k):
    pairs = []
    for f in range(far):
        for a in range(NEAR):
            for col in range(cols):
                b, g = a ^ k, f
                if col % 2 and (a < 2) != (b < 2):
                    g = (f + (1 if a >= 2 else -1)) % far
                pairs.append(((f * NEAR + a) * cols + col, (g * NEAR + b) * cols + col))
    return pairs


def collect(block, count, axis):
    return exchange(jnp.broadcast_to(block[None], (count, *block.shape)), axis)


def on_device(far, cols, momentum, gradient, right_prev):
    near = NEAR
    rows, width = momentum.shape
    rank = right_prev.shape[1]
    depth, full_width = far * near * rows, cols * width
    step, part = rank // (far * near), rank // cols
    merged = momentum + gradient.astype(jnp.float32)

    local = dot(right_prev, merged, (0, 1))
    block = exchange(local.reshape(cols, part, rows), COL).sum(0)
    left = collect(block, cols, COL).reshape(rank, rows)

    gram_block = dot(block, left, (1, 1))
    raw = dot(left, merged, (1, 0)).reshape(near, far * step, width)
    extra = jnp.pad(gram_block, ((0, 0), (0, width - rank)))
    mine = lax.axis_index(NEAR_AXIS)

    def block_for(k):
        chosen = lax.dynamic_index_in_dim(raw, jnp.bitwise_xor(mine, k), 0, keepdims=False)
        return jnp.concatenate([chosen, extra], axis=0)

    got = block_for(0)
    for came in [lax.ppermute(block_for(k), AXES, near_pairs(far, cols, k)) for k in (2, 3, 1)]:
        got = got + came
    raw = got[: far * step].reshape(far, step, width)
    gram_block = got[far * step :, :rank]
    sent = jnp.concatenate([raw, jnp.broadcast_to(gram_block[None], (far, part, rank))], axis=2)
    got = exchange(sent, FAR_AXIS).sum(0)
    raw_block, gram_block = got[:, :width], got[:, width:]
    gram = lax.all_gather(gram_block, COL, axis=0, tiled=True)
    raw = collect(raw_block, far, FAR_AXIS).reshape(far * step, width)
    halves = in_vmem(first_kernel, [(128, 128)] * 3, gram)
    raw = [raw] + [lax.ppermute(raw, AXES, near_pairs(far, cols, k)) for k in (1, 2, 3)]
    (inverse,) = in_vmem(second_kernel, [(rank, rank)], *halves)

    ortho = dot(inverse, left, (0, 0))
    parts = inverse.reshape(near, far * step, rank)
    ordered = [lax.dynamic_index_in_dim(parts, jnp.bitwise_xor(mine, k), 0, keepdims=False) for k in range(near)]
    right = dot(jnp.concatenate(raw, axis=0), jnp.concatenate(ordered, axis=0), (0, 0))
    colsq = collect(jnp.sum(right * right, axis=0, keepdims=True), cols, COL).sum(0)
    right_next = right * lax.rsqrt(colsq / full_width + 1e-06)
    new_momentum = merged - 0.05 * dot(ortho, right, (0, 1), lax.Precision.HIGH)
    factor = jnp.sqrt(jnp.float32(depth) / jnp.float32(rank))
    update = (factor * dot(ortho, right_next, (0, 1), lax.Precision.HIGH)).astype(jnp.bfloat16)
    return (new_momentum, right_next, update)


def solution(mesh):
    row, cols = mesh.devices.shape
    far = row // NEAR
    split = Mesh(mesh.devices.reshape(far, NEAR, cols), (FAR_AXIS, NEAR_AXIS, COL))
    both = P((FAR_AXIS, NEAR_AXIS), COL)
    side = P(COL, None)

    def step(momentum, gradient, right_prev):
        return on_device(far, cols, momentum, gradient, right_prev)

    return jax.shard_map(step, mesh=split, in_specs=(both, both, side), out_specs=(both, side, both), check_vma=False)
```
